32 devices in a mesh: dp: 8 (over z, y), tensor: 4 (over x, core).
Axes of the slice: x: 2, y: 2, z: 4, core: 2. Of those that a mesh axis runs over, the one named last changes fastest.
Arguments:
- layer_input: bfloat16 [2048, 768], P('dp'), may hold values from -6 to 6
- encoder_states: bfloat16 [2048, 768], P('dp'), may hold values from -6 to 6
- output_grad: bfloat16 [2048, 768], P('dp'), may hold values from -6 to 6
- segments: int32 [8, 256], P('dp'), may hold values from 0 to 7, never falling along the last dimension, each value on 1 to 128 neighbouring positions
- buckets: int32 [256], replicated, may hold values from 0 to 31
- bias_table: bfloat16 [32, 12], P(None, 'tensor'), may hold values from -4 to 4
- gain_self: float32 [768], replicated, may hold values from 0.25 to 1.75
- self_query: bfloat16 [768, 768], P(None, 'tensor'), may hold values from -0.02734375 to 0.02734375
- self_key: bfloat16 [768, 768], P(None, 'tensor'), may hold values from -0.21875 to 0.21875
- self_value: bfloat16 [768, 768], P(None, 'tensor'), may hold values from -0.21875 to 0.21875
- self_out: bfloat16 [768, 768], P('tensor'), may hold values from -0.4375 to 0.4375
- gain_cross: float32 [768], replicated, may hold values from 0.25 to 1.75
- cross_query: bfloat16 [768, 768], P(None, 'tensor'), may hold values from -0.02734375 to 0.02734375
- cross_key: bfloat16 [768, 768], P(None, 'tensor'), may hold values from -0.21875 to 0.21875
- cross_value: bfloat16 [768, 768], P(None, 'tensor'), may hold values from -0.21875 to 0.21875
- cross_out: bfloat16 [768, 768], P('tensor'), may hold values from -0.4375 to 0.4375
- gain_ff: float32 [768], replicated, may hold values from 0.25 to 1.75
- ff_gate: bfloat16 [768, 2048], P(None, 'tensor'), may hold values from -0.21875 to 0.21875
- ff_up: bfloat16 [768, 2048], P(None, 'tensor'), may hold values from -0.21875 to 0.21875
- ff_down: bfloat16 [2048, 768], P('tensor'), may hold values from -0.125 to 0.125
Outputs:
- layer_output: bfloat16 [2048, 768], P('dp', 'tensor')
- d_layer_input: float32 [2048, 768], P('dp')
- d_encoder_states: float32 [2048, 768], P('dp', 'tensor')
- d_bias_table: float32 [32, 12], P(None, 'tensor')
- d_gain_self: float32 [768], P('dp')
- d_self_query: float32 [768, 768], P('dp', 'tensor')
- d_self_key: float32 [768, 768], P('dp', 'tensor')
- d_self_value: float32 [768, 768], P('dp', 'tensor')
- d_self_out: float32 [768, 768], P('tensor', 'dp')
- d_gain_cross: float32 [768], P('dp')
- d_cross_query: float32 [768, 768], P('dp', 'tensor')
- d_cross_key: float32 [768, 768], P('dp', 'tensor')
- d_cross_value: float32 [768, 768], P('dp', 'tensor')
- d_cross_out: float32 [768, 768], P('tensor', 'dp')
- d_gain_ff: float32 [768], P('dp')
- d_ff_gate: float32 [768, 2048], P('dp', 'tensor')
- d_ff_up: float32 [768, 2048], P('dp', 'tensor')
- d_ff_down: float32 [2048, 768], P('tensor', 'dp')
The draws below stay inside these ranges and needn't reach their ends.
All inputs are finite; a program needn't handle non-finite values.
Results may differ from the reference program's by a relative error of at most 0.029.
Values sent between devices are 32-bit elements; how exact they have to be, the bound alone decides.
No kernel may reach another device: no remote copies, remote signals or barrier semaphores. Data moves between devices by JAX's collectives and lax.ppermute only.
A program may use at most 128 MiB of HBM per device.

```python
import math
import jax
import jax.numpy as jnp
import numpy as np
from jax import lax

D = 768
HEADS = 12
HEAD_DIM = 64
FF = 2048
BUCKETS = 32
SEQ = 256
HD = 768
SEQS = 8
TOKENS = 2048
ENC_TOKENS = 2048


def set_ends(drawn, rng, low, largest):
    spot = [jax.random.randint(jax.random.fold_in(rng, axis), (), 0, length) for axis, length in enumerate(drawn.shape)]
    longest = drawn.shape.index(max(drawn.shape))
    beside = spot[:longest] + [(spot[longest] + 1) % drawn.shape[longest]] + spot[longest + 1:]
    return drawn.at[tuple(spot)].set(low).at[tuple(beside)].set(largest)


def strengthened(drawn, own_key, source, target, shards_of, factor):
    def block_of(axis_at):
        return (jnp.arange(drawn.shape[axis_at]) // (drawn.shape[axis_at] // shards_of)).reshape((-1,) + (1,) * (drawn.ndim - 1 - axis_at))

    near = jax.random.permutation(own_key, shards_of)[block_of(target)]
    other_side = (block_of(target) + shards_of // 2) % shards_of
    return jnp.where((block_of(source) == near) | (block_of(source) == other_side), factor * drawn, drawn)


def block_scale(own_key, extent, pieces, low, largest):
    def one(dim, shards_of):
        steps = jax.random.uniform(jax.random.fold_in(jax.random.fold_in(own_key, 6), dim), (shards_of,), jnp.float32, low / len(pieces), largest / len(pieces))
        return jnp.repeat(jnp.exp(steps), extent[dim] // shards_of).reshape((-1,) + (1,) * (len(extent) - dim - 1))

    loudness = one(*pieces[0])
    for cut in pieces[1:]:
        loudness = loudness * one(*cut)
    return loudness


def split_up(count, total, bound, lean):
    weights = [(1 << 20) // math.isqrt(standing ** lean) + 1 for standing in range(2, count + 1)]
    surplus, given = total - bound - (count - 1), [1] * (count - 1)
    while surplus > 0:
        movable = [i for i in range(count - 1) if given[i] < bound]
        whole, budget = sum([weights[i] for i in movable]), surplus
        for i in movable:
            addition = min(bound - given[i], max(1, budget * weights[i] // whole), surplus)
            given[i] = given[i] + addition
            surplus = surplus - addition
    return np.array([bound] + given)


def uneven(rng, amount, total, limit, slope):
    if amount == 2:
        one = jax.random.randint(rng, (), max(1, total - limit), min(limit, total - 1) + 1)
        return jnp.stack([one, total - one])
    sizes = jnp.asarray(split_up(amount, total, limit, slope), jnp.int32)
    couples = (amount - 1) // 2
    donor, sink = sizes[1:1 + 2 * couples:2], sizes[2:2 + 2 * couples:2]
    slack = jnp.minimum(donor - 1, limit - sink)
    passed = jax.random.randint(jax.random.fold_in(rng, 1), (couples,), 0, 1 << 20) % (slack + 1)
    sizes = sizes.at[1:1 + 2 * couples:2].set(donor - passed).at[2:2 + 2 * couples:2].set(sink + passed)
    return sizes[jax.random.permutation(jax.random.fold_in(rng, 2), amount)]


def normal_values(key, dims, scale, most, cuts=(), held_as=jnp.bfloat16):
    entries = scale * jax.random.normal(key, dims, jnp.float32)
    if cuts:
        entries = entries * block_scale(key, dims, cuts, -0.22, 0.18)
    return jnp.clip(entries, -most, most).astype(held_as)


def gaussian_with(key, extent, spread, limit, split, heavy, kind=jnp.bfloat16):
    array = spread * jax.random.normal(key, extent, jnp.float32)
    if split:
        array = array * block_scale(key, extent, split, -0.22, 0.18)
    return jnp.clip(strengthened(array, jax.random.fold_in(key, 3), *heavy), -limit, limit).astype(kind)


def setup_inputs(seed: int = 0) -> dict:
    key_of = jax.random.split(jax.random.key(seed), 21)
    return {
        "layer_input": gaussian_with(key_of[0], (TOKENS, D), 1.0, 6.0, ((0, 8),), (0, 1, 8, 2.0)),
        "encoder_states": gaussian_with(key_of[1], (ENC_TOKENS, D), 1.0, 6.0, ((0, 8),), (0, 1, 8, 2.0)),
        "output_grad": gaussian_with(key_of[2], (TOKENS, D), 1.0, 6.0, ((0, 8),), (0, 1, 8, 2.0)),
        "segments": jax.vmap(lambda own: jnp.searchsorted(jnp.cumsum(uneven(own, 8, SEQ, SEQ // 2, 1)), jnp.arange(SEQ), side="right"))(jax.random.split(key_of[3], SEQS)).reshape((SEQS, SEQ)).astype(jnp.int32),
        "buckets": set_ends(jax.random.randint(key_of[4], (SEQ,), 0, BUCKETS), jax.random.fold_in(key_of[4], 1), 0, BUCKETS - 1).astype(jnp.int32),
        "bias_table": normal_values(key_of[5], (BUCKETS, HEADS), 1.0, 4.0, ((1, 4),)),
        "gain_self": jnp.clip(1.0 + 0.15 * jax.random.normal(key_of[6], (D,), jnp.float32), 0.25, 1.75),
        "self_query": normal_values(key_of[7], (D, HD), (D * HEAD_DIM) ** -0.5, 0.02734375, ((1, 4),)),
        "self_key": normal_values(key_of[8], (D, HD), D ** -0.5, 0.21875, ((1, 4),)),
        "self_value": normal_values(key_of[9], (D, HD), D ** -0.5, 0.21875, ((1, 4),)),
        "self_out": normal_values(key_of[10], (HD, D), (HD // 4) ** -0.5, 0.4375, ((0, 4),)),
        "gain_cross": jnp.clip(1.0 + 0.15 * jax.random.normal(key_of[11], (D,), jnp.float32), 0.25, 1.75),
        "cross_query": normal_values(key_of[12], (D, HD), (D * HEAD_DIM) ** -0.5, 0.02734375, ((1, 4),)),
        "cross_key": normal_values(key_of[13], (D, HD), D ** -0.5, 0.21875, ((1, 4),)),
        "cross_value": normal_values(key_of[14], (D, HD), D ** -0.5, 0.21875, ((1, 4),)),
        "cross_out": normal_values(key_of[15], (HD, D), (HD // 4) ** -0.5, 0.4375, ((0, 4),)),
        "gain_ff": jnp.clip(1.0 + 0.15 * jax.random.normal(key_of[16], (D,), jnp.float32), 0.25, 1.75),
        "ff_gate": normal_values(key_of[17], (D, FF), D ** -0.5, 0.21875, ((1, 4),)),
        "ff_up": normal_values(key_of[18], (D, FF), D ** -0.5, 0.21875, ((1, 4),)),
        "ff_down": normal_values(key_of[19], (FF, D), FF ** -0.5, 0.125, ((0, 4),)),
    }


epsilon = 1e-06
masked_value = -1000000000.0

def rms_norm(values, gain_vec):
    return values * lax.rsqrt(lax.optimization_barrier(jnp.mean(values * values, axis=-1, keepdims=True)) + epsilon) * gain_vec

def gelu_tanh(values):
    return jax.nn.gelu(values, approximate=True)

def product(left, right):
    return jnp.dot(left, right, preferred_element_type=jnp.float32)

def product_left(left, right):
    return jnp.dot(left.T, right, preferred_element_type=jnp.float32)

def product_right(left, right):
    return jnp.dot(left, right.T, preferred_element_type=jnp.float32)

def layout(segment_row, row_count):
    position = jnp.arange(row_count, dtype=jnp.int32)
    offset = position[:, None] - position[None, :]
    allowed = (offset >= 0) & (segment_row[:, None] == segment_row[None, :])
    return (jnp.maximum(offset, 0).astype(jnp.int32), allowed)

def offset_table(buckets, bias_table):
    onehot = (buckets[:, None] == jnp.arange(bias_table.shape[0], dtype=jnp.int32)[None, :]).astype(jnp.float32)
    return (onehot, jnp.dot(onehot, bias_table.astype(jnp.float32), precision=lax.Precision.HIGHEST))

def scores_of(query, key_rows, pos_bias, allowed):
    query_h = query.reshape(query.shape[0], HEADS, -1).astype(jnp.float32)
    key_h = key_rows.reshape(key_rows.shape[0], HEADS, -1).astype(jnp.float32)
    scores = jnp.einsum('qhd,khd->hqk', query_h, key_h)
    if pos_bias is not None:
        scores = scores + pos_bias
    if allowed is not None:
        scores = jnp.where(allowed[None], scores, masked_value)
    return scores

def attend(query, key_rows, values, pos_bias, allowed):
    scores = scores_of(query, key_rows, pos_bias, allowed)
    row_top = lax.optimization_barrier(jnp.max(scores, axis=-1, keepdims=True))
    exp_scores = jnp.exp(scores - row_top)
    exp_total = lax.optimization_barrier(jnp.sum(exp_scores, axis=-1, keepdims=True))
    weights = (exp_scores / exp_total).astype(jnp.bfloat16)
    value_h = values.reshape(values.shape[0], HEADS, -1)
    mixed = jnp.einsum('hqk,khd->qhd', weights.astype(jnp.float32), value_h.astype(jnp.float32))
    return (mixed.reshape(query.shape[0], -1).astype(jnp.bfloat16), row_top + jnp.log(exp_total))

def attend_back(query, key_rows, values, mixed, d_mixed, lse_rows, pos_bias, allowed):
    scores = scores_of(query, key_rows, pos_bias, allowed)
    prob_rows = jnp.exp(scores - lse_rows)
    row_count = query.shape[0]
    query_h = query.reshape(row_count, HEADS, -1).astype(jnp.float32)
    key_h = key_rows.reshape(key_rows.shape[0], HEADS, -1).astype(jnp.float32)
    value_h = values.reshape(values.shape[0], HEADS, -1).astype(jnp.float32)
    dmix_h = d_mixed.reshape(row_count, HEADS, -1).astype(jnp.float32)
    mix_h = mixed.reshape(row_count, HEADS, -1).astype(jnp.float32)
    d_probs = jnp.einsum('qhd,khd->hqk', dmix_h, value_h)
    delta_rows = jnp.transpose(lax.optimization_barrier(jnp.sum(dmix_h * mix_h, axis=-1)))[:, :, None]
    d_scores = prob_rows * (d_probs - delta_rows)
    d_weights = d_scores.astype(jnp.bfloat16).astype(jnp.float32)
    d_query = jnp.einsum('hqk,khd->qhd', d_weights, key_h).reshape(row_count, -1).astype(jnp.bfloat16)
    d_keys = jnp.einsum('hqk,qhd->khd', d_weights, query_h).reshape(key_rows.shape[0], -1).astype(jnp.bfloat16)
    d_values = jnp.einsum('hqk,qhd->khd', prob_rows.astype(jnp.bfloat16).astype(jnp.float32), dmix_h).reshape(key_rows.shape[0], -1).astype(jnp.bfloat16)
    return (d_query, d_keys, d_values, d_scores)

def norm_back(values, gain_vec, cotangent):
    unused, pull_back = jax.vjp(rms_norm, values, gain_vec)
    return pull_back(cotangent)

def sequence_pass(weights, x_rows, enc_rows, dy_rows, segment_row, buckets):
    bias_table, gain_self, self_query, self_key, self_value, self_out, gain_cross, cross_query, cross_key, cross_value, cross_out, gain_ff, ff_gate, ff_up, ff_down = weights
    row_count = x_rows.shape[0]
    stream_in = x_rows.astype(jnp.float32)
    offset, allowed = layout(segment_row, row_count)
    onehot, per_offset = offset_table(buckets, bias_table)
    pos_bias = jnp.transpose(per_offset[offset], (2, 0, 1))
    normed_self = rms_norm(stream_in, gain_self).astype(jnp.bfloat16)
    self_q = product(normed_self, self_query).astype(jnp.bfloat16)
    self_k = product(normed_self, self_key).astype(jnp.bfloat16)
    self_v = product(normed_self, self_value).astype(jnp.bfloat16)
    mix_self, lse_self = attend(self_q, self_k, self_v, pos_bias, allowed)
    resid_one = stream_in + product(mix_self, self_out)
    normed_cross = rms_norm(resid_one, gain_cross).astype(jnp.bfloat16)
    cross_q = product(normed_cross, cross_query).astype(jnp.bfloat16)
    cross_k = product(enc_rows, cross_key).astype(jnp.bfloat16)
    cross_v = product(enc_rows, cross_value).astype(jnp.bfloat16)
    mix_cross, lse_cross = attend(cross_q, cross_k, cross_v, None, None)
    resid_two = resid_one + product(mix_cross, cross_out)
    normed_ff = rms_norm(resid_two, gain_ff).astype(jnp.bfloat16)
    gate_pre = product(normed_ff, ff_gate)
    up_pre = product(normed_ff, ff_up)
    activ, gelu_pull = jax.vjp(gelu_tanh, gate_pre)
    hidden = (activ * up_pre).astype(jnp.bfloat16)
    out_rows = (resid_two + product(hidden, ff_down)).astype(jnp.bfloat16)
    grad_out = dy_rows.astype(jnp.float32)
    d_ff_down = product_left(hidden, dy_rows)
    d_hidden = product_right(dy_rows, ff_down)
    d_gate_pre = gelu_pull(d_hidden * up_pre)[0].astype(jnp.bfloat16)
    d_up_pre = (d_hidden * activ).astype(jnp.bfloat16)
    d_ff_gate = product_left(normed_ff, d_gate_pre)
    d_ff_up = product_left(normed_ff, d_up_pre)
    d_normed_ff = product_right(d_gate_pre, ff_gate) + product_right(d_up_pre, ff_up)
    d_resid, d_gain_ff = norm_back(resid_two, gain_ff, d_normed_ff)
    grad_two = grad_out + d_resid
    grad_two_b = grad_two.astype(jnp.bfloat16)
    d_cross_out = product_left(mix_cross, grad_two_b)
    d_mix_cross = product_right(grad_two_b, cross_out).astype(jnp.bfloat16)
    d_cross_q, d_cross_k, d_cross_v, unused = attend_back(cross_q, cross_k, cross_v, mix_cross, d_mix_cross, lse_cross, None, None)
    d_cross_query = product_left(normed_cross, d_cross_q)
    d_cross_key = product_left(enc_rows, d_cross_k)
    d_cross_value = product_left(enc_rows, d_cross_v)
    d_enc_rows = product_right(d_cross_k, cross_key) + product_right(d_cross_v, cross_value)
    d_normed_cross = product_right(d_cross_q, cross_query)
    d_resid, d_gain_cross = norm_back(resid_one, gain_cross, d_normed_cross)
    grad_one = grad_two + d_resid
    grad_one_b = grad_one.astype(jnp.bfloat16)
    d_self_out = product_left(mix_self, grad_one_b)
    d_mix_self = product_right(grad_one_b, self_out).astype(jnp.bfloat16)
    d_self_q, d_self_k, d_self_v, ds_self = attend_back(self_q, self_k, self_v, mix_self, d_mix_self, lse_self, pos_bias, allowed)
    flat_scores = jnp.transpose(ds_self, (1, 2, 0)).reshape(row_count * row_count, HEADS)
    by_offset = jax.ops.segment_sum(flat_scores, offset.reshape(-1), num_segments=row_count)
    d_bias_table = jnp.dot(onehot.T, by_offset, precision=lax.Precision.HIGHEST)
    d_self_query = product_left(normed_self, d_self_q)
    d_self_key = product_left(normed_self, d_self_k)
    d_self_value = product_left(normed_self, d_self_v)
    d_normed_self = product_right(d_self_q, self_query) + product_right(d_self_k, self_key) + product_right(d_self_v, self_value)
    d_resid, d_gain_self = norm_back(stream_in, gain_self, d_normed_self)
    d_x_rows = grad_one + d_resid
    grads = (d_bias_table, d_gain_self, d_self_query, d_self_key, d_self_value, d_self_out, d_gain_cross, d_cross_query, d_cross_key, d_cross_value, d_cross_out, d_gain_ff, d_ff_gate, d_ff_up, d_ff_down)
    return (out_rows, d_x_rows, d_enc_rows, grads)

def reference(layer_input, encoder_states, output_grad, segments, buckets, bias_table, gain_self, self_query, self_key, self_value, self_out, gain_cross, cross_query, cross_key, cross_value, cross_out, gain_ff, ff_gate, ff_up, ff_down):
    weights = (bias_table, gain_self, self_query, self_key, self_value, self_out, gain_cross, cross_query, cross_key, cross_value, cross_out, gain_ff, ff_gate, ff_up, ff_down)
    row_count = segments.shape[1]
    x_seq = layer_input.reshape(-1, row_count, layer_input.shape[1])
    dy_seq = output_grad.reshape(-1, row_count, output_grad.shape[1])
    enc_seq = encoder_states.reshape(x_seq.shape[0], -1, encoder_states.shape[1])
    zero_grads = tuple((jnp.zeros(weight.shape, jnp.float32) for weight in weights))

    def seq_step(carried, seq_item):
        x_rows, enc_rows, dy_rows, segment_row = seq_item
        out_rows, d_x_rows, d_enc_rows, grads = sequence_pass(weights, x_rows, enc_rows, dy_rows, segment_row, buckets)
        carried = tuple((left_sum + right_sum for left_sum, right_sum in zip(carried, grads)))
        return (carried, (out_rows, d_x_rows, d_enc_rows))
    totals, stacked = lax.scan(seq_step, zero_grads, (x_seq, enc_seq, dy_seq, segments))
    layer_output = stacked[0].reshape(layer_input.shape)
    d_layer_input = stacked[1].reshape(layer_input.shape)
    d_encoder_states = stacked[2].reshape(encoder_states.shape)
    return (layer_output, d_layer_input, d_encoder_states) + totals
```

```python
import jax
import jax.numpy as jnp
from jax import lax
from jax.sharding import PartitionSpec as P

epsilon = 1e-06
masked_value = -1000000000.0


def rms_norm(values, gain_vec):
    return (
        values * lax.rsqrt(jnp.mean(values * values, axis=-1, keepdims=True) + epsilon) * gain_vec
    )


def gelu_tanh(values):
    return jax.nn.gelu(values, approximate=True)


def product(left, right):
    return jnp.dot(left, right, preferred_element_type=jnp.float32)


def product_left(left, right):
    return lax.dot_general(
        left, right, (((0,), (0,)), ((), ())), preferred_element_type=jnp.float32
    )


def product_right(left, right):
    return lax.dot_general(
        left, right, (((1,), (1,)), ((), ())), preferred_element_type=jnp.float32
    )


def allowed_pairs(segment_row, row_count):
    position = jnp.arange(row_count, dtype=jnp.int32)
    causal = position[:, None] >= position[None, :]
    return causal & (segment_row[:, None] == segment_row[None, :])


def offset_table(buckets, bias_table):
    onehot = (buckets[:, None] == jnp.arange(bias_table.shape[0], dtype=jnp.int32)[None, :]).astype(
        jnp.float32
    )
    return (
        onehot,
        jnp.dot(onehot, bias_table.astype(jnp.float32), precision=lax.Precision.HIGHEST),
    )


def spread_diagonals(per_offset, row_count):
    head_count = per_offset.shape[1]
    pattern = jnp.concatenate(
        [
            jnp.flip(jnp.transpose(per_offset), axis=1),
            jnp.zeros((head_count, row_count), jnp.float32),
        ],
        axis=1,
    )
    width = 2 * row_count - 1
    tiled = jnp.tile(pattern, (1, row_count))[:, : row_count * width]
    return tiled.reshape(head_count, row_count, width)[:, :, row_count - 1 :]


def sum_diagonals(d_scores, row_count):
    head_count = d_scores.shape[0]
    width = 2 * row_count - 1
    placed = jnp.concatenate(
        [jnp.zeros((head_count, row_count, row_count - 1), jnp.float32), d_scores], axis=2
    )
    flat = placed.reshape(head_count, row_count * width)
    flat = jnp.concatenate([flat, jnp.zeros((head_count, row_count), jnp.float32)], axis=1)
    folded = jnp.sum(flat.reshape(head_count, row_count, 2 * row_count), axis=1)
    return jnp.transpose(jnp.flip(folded[:, :row_count], axis=1))


def scores_of(query, key_rows, head_count, pos_bias, allowed):
    query_h = query.reshape(query.shape[0], head_count, -1)
    key_h = key_rows.reshape(key_rows.shape[0], head_count, -1)
    scores = jnp.einsum("qhd,khd->hqk", query_h, key_h, preferred_element_type=jnp.float32)
    if pos_bias is not None:
        scores = scores + pos_bias
    if allowed is not None:
        scores = jnp.where(allowed[None], scores, masked_value)
    return scores


def attend(query, key_rows, values, head_count, pos_bias, allowed):
    scores = scores_of(query, key_rows, head_count, pos_bias, allowed)
    row_top = jnp.max(scores, axis=-1, keepdims=True)
    exp_scores = jnp.exp(scores - row_top)
    exp_total = jnp.sum(exp_scores, axis=-1, keepdims=True)
    weights = (exp_scores / exp_total).astype(jnp.bfloat16)
    value_h = values.reshape(values.shape[0], head_count, -1)
    mixed = jnp.einsum("hqk,khd->qhd", weights, value_h, preferred_element_type=jnp.float32)
    return (mixed.reshape(query.shape[0], -1).astype(jnp.bfloat16), row_top + jnp.log(exp_total))


def attend_back(query, key_rows, values, mixed, d_mixed, lse_rows, head_count, pos_bias, allowed):
    scores = scores_of(query, key_rows, head_count, pos_bias, allowed)
    prob_rows = jnp.exp(scores - lse_rows)
    row_count = query.shape[0]
    query_h = query.reshape(row_count, head_count, -1)
    key_h = key_rows.reshape(key_rows.shape[0], head_count, -1)
    value_h = values.reshape(values.shape[0], head_count, -1)
    dmix_h = d_mixed.reshape(row_count, head_count, -1)
    mix_h = mixed.reshape(row_count, head_count, -1)
    d_probs = jnp.einsum("qhd,khd->hqk", dmix_h, value_h, preferred_element_type=jnp.float32)
    delta_rows = jnp.transpose(
        jnp.sum(dmix_h.astype(jnp.float32) * mix_h.astype(jnp.float32), axis=-1)
    )[:, :, None]
    d_scores = prob_rows * (d_probs - delta_rows)
    d_weights = d_scores.astype(jnp.bfloat16)
    d_query = jnp.einsum("hqk,khd->qhd", d_weights, key_h, preferred_element_type=jnp.float32)
    d_keys = jnp.einsum("hqk,qhd->khd", d_weights, query_h, preferred_element_type=jnp.float32)
    d_values = jnp.einsum(
        "hqk,qhd->khd", prob_rows.astype(jnp.bfloat16), dmix_h, preferred_element_type=jnp.float32
    )
    return (
        d_query.reshape(row_count, -1).astype(jnp.bfloat16),
        d_keys.reshape(key_rows.shape[0], -1).astype(jnp.bfloat16),
        d_values.reshape(key_rows.shape[0], -1).astype(jnp.bfloat16),
        d_scores,
    )


def norm_back(values, gain_vec, cotangent):
    unused, pull_back = jax.vjp(rms_norm, values, gain_vec)
    return pull_back(cotangent)


def swap_pairs(count, stride):
    return [(i, i ^ stride) for i in range(count)]


def power_of_two(count):
    return count > 1 and count & (count - 1) == 0


def pick_half(values, bit, axis):
    half = values.shape[axis] // 2
    return lax.dynamic_slice_in_dim(values, bit * half, half, axis)


def tensor_sum(partial_rows):
    count = lax.axis_size("tensor")
    if not power_of_two(count):
        return lax.psum(partial_rows, "tensor")
    bit = lax.axis_index("tensor") & 1
    total = pick_half(partial_rows, bit, 0) + lax.ppermute(
        pick_half(partial_rows, 1 - bit, 0), "tensor", swap_pairs(count, 1)
    )
    stride = 2
    while stride < count:
        total = total + lax.ppermute(total, "tensor", swap_pairs(count, stride))
        stride *= 2
    other = lax.ppermute(total, "tensor", swap_pairs(count, 1))
    first = jnp.where(bit == 0, total, other)
    second = jnp.where(bit == 0, other, total)
    return jnp.concatenate([first, second], axis=0)


def scatter_blocks(blocks, axis_name, bits):
    count = lax.axis_size(axis_name)
    index = lax.axis_index(axis_name)
    remaining = list(range(count.bit_length() - 1))
    shape = blocks.shape[1:]
    for bit in bits:
        place = remaining.index(bit)
        low = 2**place
        high = 2 ** (len(remaining) - 1 - place)
        mine = (index >> bit) & 1
        view = blocks.reshape((high, 2, low) + shape)
        keep = lax.dynamic_index_in_dim(view, mine, 1, keepdims=False)
        send = lax.dynamic_index_in_dim(view, 1 - mine, 1, keepdims=False)
        received = lax.ppermute(send, axis_name, swap_pairs(count, 2**bit))
        blocks = (keep + received).reshape((high * low,) + shape)
        remaining.remove(bit)
    return blocks[0]


def scatter_sum(blocks, axis_name, low_first):
    count = lax.axis_size(axis_name)
    if not power_of_two(count):
        return lax.psum_scatter(blocks, axis_name, scatter_dimension=0, tiled=False)
    bits = list(range(count.bit_length() - 1))
    if not low_first:
        bits = bits[1:] + bits[:1]
    return scatter_blocks(blocks, axis_name, bits)


def row_scatter(grad_rows, low_first=True):
    count = lax.axis_size("dp")
    return scatter_sum(
        grad_rows.reshape(count, grad_rows.shape[0] // count, grad_rows.shape[1]), "dp", low_first
    )


def column_scatter(partial_rows):
    count = lax.axis_size("tensor")
    width = partial_rows.shape[1] // count
    blocks = jnp.stack([partial_rows[:, i * width : (i + 1) * width] for i in range(count)])
    return scatter_sum(blocks, "tensor", True)


def on_device(
    layer_input,
    encoder_states,
    output_grad,
    segments,
    buckets,
    bias_table,
    gain_self,
    self_query,
    self_key,
    self_value,
    self_out,
    gain_cross,
    cross_query,
    cross_key,
    cross_value,
    cross_out,
    gain_ff,
    ff_gate,
    ff_up,
    ff_down,
):
    heads_local = bias_table.shape[1]
    row_count = layer_input.shape[0]
    stream_in = layer_input.astype(jnp.float32)
    allowed = allowed_pairs(segments[0], row_count)
    onehot, per_offset = offset_table(buckets, bias_table)
    pos_bias = spread_diagonals(per_offset, row_count)
    normed_self = rms_norm(stream_in, gain_self).astype(jnp.bfloat16)
    self_q = product(normed_self, self_query).astype(jnp.bfloat16)
    self_k = product(normed_self, self_key).astype(jnp.bfloat16)
    self_v = product(normed_self, self_value).astype(jnp.bfloat16)
    mix_self, lse_self = attend(self_q, self_k, self_v, heads_local, pos_bias, allowed)
    resid_one = stream_in + tensor_sum(product(mix_self, self_out))
    normed_cross = rms_norm(resid_one, gain_cross).astype(jnp.bfloat16)
    cross_q = product(normed_cross, cross_query).astype(jnp.bfloat16)
    cross_k = product(encoder_states, cross_key).astype(jnp.bfloat16)
    cross_v = product(encoder_states, cross_value).astype(jnp.bfloat16)
    mix_cross, lse_cross = attend(cross_q, cross_k, cross_v, heads_local, None, None)
    resid_two = resid_one + tensor_sum(product(mix_cross, cross_out))
    normed_ff = rms_norm(resid_two, gain_ff).astype(jnp.bfloat16)
    gate_pre = product(normed_ff, ff_gate)
    up_pre = product(normed_ff, ff_up)
    activ, gelu_pull = jax.vjp(gelu_tanh, gate_pre)
    hidden = (activ * up_pre).astype(jnp.bfloat16)
    grad_out = output_grad.astype(jnp.float32)
    d_hidden = product_right(output_grad, ff_down)
    d_gate_pre = gelu_pull(d_hidden * up_pre)[0].astype(jnp.bfloat16)
    d_up_pre = (d_hidden * activ).astype(jnp.bfloat16)
    d_normed_ff = tensor_sum(product_right(d_gate_pre, ff_gate) + product_right(d_up_pre, ff_up))
    ff_share = column_scatter(product(hidden, ff_down))
    col_width = ff_share.shape[1]
    resid_cols = lax.dynamic_slice_in_dim(
        resid_two, lax.axis_index("tensor") * col_width, col_width, 1
    )
    layer_output = (resid_cols + ff_share).astype(jnp.bfloat16)
    down_rows = row_scatter(product_left(output_grad, hidden), False)
    gate_rows = row_scatter(product_left(normed_ff, d_gate_pre))
    up_rows = row_scatter(product_left(normed_ff, d_up_pre))
    d_resid, d_gain_ff = norm_back(resid_two, gain_ff, d_normed_ff)
    grad_two = grad_out + d_resid
    grad_two_b = grad_two.astype(jnp.bfloat16)
    d_mix_cross = product_right(grad_two_b, cross_out).astype(jnp.bfloat16)
    d_cross_q, d_cross_k, d_cross_v, unused = attend_back(
        cross_q, cross_k, cross_v, mix_cross, d_mix_cross, lse_cross, heads_local, None, None
    )
    d_normed_cross = tensor_sum(product_right(d_cross_q, cross_query))
    cross_rows = row_scatter(
        jnp.concatenate(
            [
                product_left(normed_cross, d_cross_q),
                product_left(encoder_states, d_cross_k),
                product_left(encoder_states, d_cross_v),
                product_left(grad_two_b, mix_cross),
            ],
            axis=1,
        )
    )
    d_encoder_states = column_scatter(
        product_right(d_cross_k, cross_key) + product_right(d_cross_v, cross_value)
    )
    d_resid, d_gain_cross = norm_back(resid_one, gain_cross, d_normed_cross)
    grad_one = grad_two + d_resid
    grad_one_b = grad_one.astype(jnp.bfloat16)
    d_mix_self = product_right(grad_one_b, self_out).astype(jnp.bfloat16)
    d_self_q, d_self_k, d_self_v, ds_self = attend_back(
        self_q, self_k, self_v, mix_self, d_mix_self, lse_self, heads_local, pos_bias, allowed
    )
    d_normed_self = tensor_sum(
        product_right(d_self_q, self_query)
        + product_right(d_self_k, self_key)
        + product_right(d_self_v, self_value)
    )
    self_rows = row_scatter(
        jnp.concatenate(
            [
                product_left(normed_self, d_self_q),
                product_left(normed_self, d_self_k),
                product_left(normed_self, d_self_v),
                product_left(grad_one_b, mix_self),
            ],
            axis=1,
        )
    )
    by_offset = sum_diagonals(ds_self, row_count)
    d_bias = jnp.dot(onehot.T, by_offset, precision=lax.Precision.HIGHEST)
    d_resid, d_gain_self = norm_back(stream_in, gain_self, d_normed_self)
    d_layer_input = grad_one + d_resid
    dp_count = lax.axis_size("dp")
    small = jnp.concatenate(
        [g.reshape(dp_count, -1) for g in (d_gain_self, d_gain_cross, d_gain_ff)]
        + [jnp.broadcast_to(d_bias.reshape(1, -1), (dp_count, d_bias.size))],
        axis=1,
    )
    small = scatter_sum(small, "dp", True)
    share = gain_self.shape[0] // dp_count
    d_bias_table = small[3 * share :].reshape(d_bias.shape)
    width = self_query.shape[1]

    def quarter(rows, i):
        return rows[:, i * width : (i + 1) * width]

    return (
        layer_output,
        d_layer_input,
        d_encoder_states,
        d_bias_table,
        small[:share],
        quarter(self_rows, 0),
        quarter(self_rows, 1),
        quarter(self_rows, 2),
        jnp.transpose(quarter(self_rows, 3)),
        small[share : 2 * share],
        quarter(cross_rows, 0),
        quarter(cross_rows, 1),
        quarter(cross_rows, 2),
        jnp.transpose(quarter(cross_rows, 3)),
        small[2 * share : 3 * share],
        gate_rows,
        up_rows,
        jnp.transpose(down_rows),
    )


def solution(mesh):
    in_specs = (
        P("dp", None),
        P("dp", None),
        P("dp", None),
        P("dp", None),
        P(),
        P(None, "tensor"),
        P(),
        P(None, "tensor"),
        P(None, "tensor"),
        P(None, "tensor"),
        P("tensor", None),
        P(),
        P(None, "tensor"),
        P(None, "tensor"),
        P(None, "tensor"),
        P("tensor", None),
        P(),
        P(None, "tensor"),
        P(None, "tensor"),
        P("tensor", None),
    )
    out_specs = (
        P("dp", "tensor"),
        P("dp", None),
        P("dp", "tensor"),
        P(None, "tensor"),
        P("dp"),
        P("dp", "tensor"),
        P("dp", "tensor"),
        P("dp", "tensor"),
        P("tensor", "dp"),
        P("dp"),
        P("dp", "tensor"),
        P("dp", "tensor"),
        P("dp", "tensor"),
        P("tensor", "dp"),
        P("dp"),
        P("dp", "tensor"),
        P("dp", "tensor"),
        P("tensor", "dp"),
    )
    return jax.shard_map(
        on_device, mesh=mesh, in_specs=in_specs, out_specs=out_specs, check_vma=False
    )
```

```python
import functools

import jax
import jax.numpy as jnp
from jax import lax
from jax.experimental import pallas as pl
from jax.experimental.pallas import tpu as pltpu
from jax.sharding import PartitionSpec as P

epsilon = 1e-06
masked_value = -1000000000.0
gelu_rate = 0.7978845608028654
gelu_cube = 0.044715
f32 = jnp.float32
bf16 = jnp.bfloat16


def product(left, right):
    return jnp.dot(left, right, preferred_element_type=f32)


def product_left(left, right):
    return lax.dot_general(left, right, (((0,), (0,)), ((), ())), preferred_element_type=f32)


def product_right(left, right):
    return lax.dot_general(left, right, (((1,), (1,)), ((), ())), preferred_element_type=f32)


def inverse_rms(values):
    return lax.rsqrt(jnp.mean(values * values, axis=-1, keepdims=True) + epsilon)


def norm_pull(values, gain_row, cotangent):
    scale = inverse_rms(values)
    weighted = cotangent * gain_row
    mean_part = jnp.mean(weighted * values, axis=-1, keepdims=True)
    d_values = scale * weighted - values * (scale * scale * scale * mean_part)
    d_gain = jnp.sum(cotangent * values * scale, axis=0, keepdims=True)
    return d_values, d_gain


def head_columns(values, head, width):
    return values[:, head * width : (head + 1) * width]


def split_halves(part_ref, send_ref, keep_ref, bit):
    half = keep_ref.shape[0]
    send_ref[...] = part_ref[pl.ds((1 - bit) * half, half), :]
    keep_ref[...] = part_ref[pl.ds(bit * half, half), :]


def join_halves(full_ref, own_ref, other_ref, bit):
    half = own_ref.shape[0]
    full_ref[pl.ds(bit * half, half), :] = own_ref[...]
    full_ref[pl.ds((1 - bit) * half, half), :] = other_ref[...]


def split_blocks(grad_ref, send_ref, keep_ref, bit):
    pairs, rows, unused = keep_ref.shape
    for pair in range(pairs):
        if rows % 8 == 0:
            start = 2 * pair * rows
            send_ref[pair] = grad_ref[pl.ds(pl.multiple_of(start + (1 - bit) * rows, 8), rows), :]
            keep_ref[pair] = grad_ref[pl.ds(pl.multiple_of(start + bit * rows, 8), rows), :]
        else:
            first = grad_ref[2 * pair * rows : (2 * pair + 1) * rows, :]
            second = grad_ref[(2 * pair + 1) * rows : (2 * pair + 2) * rows, :]
            send_ref[pair] = jnp.where(bit == 0, second, first)
            keep_ref[pair] = jnp.where(bit == 0, first, second)


def softmax_rows(scores):
    exp_scores = jnp.exp(scores - jnp.max(scores, axis=-1, keepdims=True))
    return exp_scores / jnp.sum(exp_scores, axis=-1, keepdims=True)


def self_forward(
    place, x_ref, gain, wq, wk, wv, wo, seg, back_buckets, table,
    normed_ref, qkv_ref, prob_ref, mix_ref, send_ref, keep_ref, part_ref,
):
    heads = table.shape[1]
    width = wq.shape[1]
    size = width // heads
    rows = x_ref.shape[0]
    x = x_ref[...].astype(f32)
    normed = (x * inverse_rms(x) * gain[...]).astype(bf16)
    normed_ref[...] = normed
    query = product(normed, wq[...]).astype(bf16)
    key_rows = product(normed, wk[...]).astype(bf16)
    values = product(normed, wv[...]).astype(bf16)
    qkv_ref[...] = jnp.concatenate([query, key_rows, values], axis=1)
    row_id = lax.broadcasted_iota(jnp.int32, (rows, rows), 0)
    col_id = lax.broadcasted_iota(jnp.int32, (rows, rows), 1)
    seg_row = seg[...]
    seg_col = jnp.sum(jnp.where(row_id == col_id, seg_row, 0), axis=1, keepdims=True)
    allowed = (row_id >= col_id) & (seg_col == seg_row)
    bucket_id = lax.broadcasted_iota(jnp.int32, (table.shape[0], rows), 0)
    hit = bucket_id == back_buckets[...]
    table_f = table[...].astype(f32)
    mixes = []
    for h in range(heads):
        pattern = jnp.sum(jnp.where(hit, table_f[:, h : h + 1], 0.0), axis=0, keepdims=True)
        bias = pltpu.roll(
            jnp.broadcast_to(pattern, (rows, rows)), 0, 1, stride=1, stride_axis=0
        )
        scores = product_right(head_columns(query, h, size), head_columns(key_rows, h, size))
        prob = softmax_rows(jnp.where(allowed, scores + bias, masked_value))
        prob_ref[h] = prob
        mixes.append(product(prob.astype(bf16), head_columns(values, h, size)))
    mix = jnp.concatenate(mixes, axis=1).astype(bf16)
    mix_ref[...] = mix
    part_ref[...] = product(mix, wo[...])
    split_halves(part_ref, send_ref, keep_ref, place[0])


def cross_forward(
    place, own, other, x_ref, gain, wq, wo, kv,
    resid_ref, normed_ref, query_ref, prob_ref, mix_ref, send_ref, keep_ref, part_ref, *, heads,
):
    width = wq.shape[1]
    size = width // heads
    join_halves(part_ref, own, other, place[0])
    resid = x_ref[...].astype(f32) + part_ref[...]
    resid_ref[...] = resid
    normed = (resid * inverse_rms(resid) * gain[...]).astype(bf16)
    normed_ref[...] = normed
    query = product(normed, wq[...]).astype(bf16)
    query_ref[...] = query
    mixes = []
    for h in range(heads):
        key_h = kv[:, h * size : (h + 1) * size]
        value_h = kv[:, width + h * size : width + (h + 1) * size]
        prob = softmax_rows(product_right(head_columns(query, h, size), key_h))
        prob_ref[h] = prob
        mixes.append(product(prob.astype(bf16), value_h))
    mix = jnp.concatenate(mixes, axis=1).astype(bf16)
    mix_ref[...] = mix
    part_ref[...] = product(mix, wo[...])
    split_halves(part_ref, send_ref, keep_ref, place[0])


def cross_key_value(enc, wk, wv, kv_ref):
    rows = enc[...]
    kv_ref[...] = jnp.concatenate(
        [product(rows, wk[...]).astype(bf16), product(rows, wv[...]).astype(bf16)], axis=1
    )


def ff_both(
    place, own, other, resid_one, gain, wg, wu, wd, out_grad,
    resid_ref, normed_ref, hidden_ref, d_pre_ref, send_ref, keep_ref, part_ref,
):
    join_halves(part_ref, own, other, place[0])
    resid = resid_one[...] + part_ref[...]
    resid_ref[...] = resid
    normed = (resid * inverse_rms(resid) * gain[...]).astype(bf16)
    normed_ref[...] = normed
    gate = product(normed, wg[...])
    up = product(normed, wu[...])
    d_hidden = product_right(out_grad[...], wd[...])
    square = gate * gate
    bend = jnp.tanh(gelu_rate * (gate + gelu_cube * (square * gate)))
    activ = 0.5 * gate * (1.0 + bend)
    slope = 0.5 * (1.0 + bend) + 0.5 * gate * (1.0 - bend * bend) * (
        gelu_rate * (1.0 + 3.0 * gelu_cube * square)
    )
    hidden_ref[...] = (activ * up).astype(bf16)
    d_gate = (d_hidden * up * slope).astype(bf16)
    d_up = (d_hidden * activ).astype(bf16)
    width = d_gate.shape[1]
    d_pre_ref[:, :width] = d_gate
    d_pre_ref[:, width:] = d_up
    part_ref[...] = product_right(d_gate, wg[...]) + product_right(d_up, wu[...])
    split_halves(part_ref, send_ref, keep_ref, place[0])


def column_pieces(part, send_ref, keep_ref, bit):
    pairs, unused, width = keep_ref.shape
    for pair in range(pairs):
        first = part[:, 2 * pair * width : (2 * pair + 1) * width]
        second = part[:, (2 * pair + 1) * width : (2 * pair + 2) * width]
        send_ref[pair] = jnp.where(bit == 0, second, first)
        keep_ref[pair] = jnp.where(bit == 0, first, second)


def ff_grads(
    place, normed, d_pre, hidden, out_grad, wd,
    send_ref, keep_ref, down_ref, out_send, out_keep, grad_ref,
):
    grad_ref[...] = product_left(normed[...], d_pre[...])
    split_blocks(grad_ref, send_ref, keep_ref, place[1])
    down = product_left(out_grad[...], hidden[...])
    blocks, rows, unused = down_ref.shape
    for block in range(blocks):
        down_ref[block] = down[block * rows : (block + 1) * rows, :]
    column_pieces(product(hidden[...], wd[...]), out_send, out_keep, place[0])


def cross_backward(
    place, own, other, resid_two, gain, out_grad, wo, wq, prob, query, kv, mix,
    grad_ref, grad_b_ref, d_gain_ref, d_mix_ref, d_score_ref, d_query_ref, send_ref, keep_ref,
    part_ref, *, heads,
):
    width = wq.shape[1]
    size = width // heads
    join_halves(part_ref, own, other, place[0])
    d_resid, d_gain = norm_pull(resid_two[...], gain[...], part_ref[...])
    d_gain_ref[...] = d_gain
    grad = out_grad[...].astype(f32) + d_resid
    grad_ref[...] = grad
    grad_b = grad.astype(bf16)
    grad_b_ref[...] = grad_b
    d_mix = product_right(grad_b, wo[...]).astype(bf16)
    d_mix_ref[...] = d_mix
    drift = d_mix.astype(f32) * mix[...].astype(f32)
    d_queries = []
    for h in range(heads):
        key_h = kv[:, h * size : (h + 1) * size]
        value_h = kv[:, width + h * size : width + (h + 1) * size]
        delta = jnp.sum(head_columns(drift, h, size), axis=1, keepdims=True)
        d_prob = product_right(head_columns(d_mix, h, size), value_h)
        d_score = (prob[h] * (d_prob - delta)).astype(bf16)
        d_score_ref[h] = d_score
        d_queries.append(product(d_score, key_h))
    d_query = jnp.concatenate(d_queries, axis=1).astype(bf16)
    d_query_ref[...] = d_query
    part_ref[...] = product_right(d_query, wq[...])
    split_halves(part_ref, send_ref, keep_ref, place[0])


def cross_grads(
    place, normed, enc, grad_b, mix, prob, query, d_mix, d_score, d_query, wk, wv,
    send_ref, keep_ref, enc_send, enc_keep, grad_ref, *, heads,
):
    width = wk.shape[1]
    size = width // heads
    d_keys = []
    d_values = []
    for h in range(heads):
        d_keys.append(product_left(d_score[h], query[:, h * size : (h + 1) * size]))
        d_values.append(product_left(prob[h].astype(bf16), d_mix[:, h * size : (h + 1) * size]))
    d_key = jnp.concatenate(d_keys, axis=1).astype(bf16)
    d_value = jnp.concatenate(d_values, axis=1).astype(bf16)
    column_pieces(
        product_right(d_key, wk[...]) + product_right(d_value, wv[...]),
        enc_send,
        enc_keep,
        place[0],
    )
    grad_ref[:, : 2 * width] = product_left(enc[...], jnp.concatenate([d_key, d_value], axis=1))
    grad_ref[:, 2 * width :] = jnp.concatenate(
        [product_left(normed[...], d_query[...]), product_left(grad_b[...], mix[...])], axis=1
    )
    split_blocks(grad_ref, send_ref, keep_ref, place[1])


def self_backward(
    place, own, other, resid_one, gain, grad_two, wo, wq, wk, wv, prob, qkv, mix,
    grad_ref, grad_b_ref, d_gain_ref, d_score_ref, d_qkv_ref, send_ref, keep_ref,
    part_ref, *, heads,
):
    width = wq.shape[1]
    size = width // heads
    join_halves(part_ref, own, other, place[0])
    d_resid, d_gain = norm_pull(resid_one[...], gain[...], part_ref[...])
    d_gain_ref[...] = d_gain
    grad = grad_two[...] + d_resid
    grad_ref[...] = grad
    grad_b = grad.astype(bf16)
    grad_b_ref[...] = grad_b
    d_mix = product_right(grad_b, wo[...]).astype(bf16)
    drift = d_mix.astype(f32) * mix[...].astype(f32)
    d_queries = []
    d_keys = []
    d_values = []
    for h in range(heads):
        query_h = qkv[:, h * size : (h + 1) * size]
        key_h = qkv[:, width + h * size : width + (h + 1) * size]
        value_h = qkv[:, 2 * width + h * size : 2 * width + (h + 1) * size]
        d_mix_h = head_columns(d_mix, h, size)
        delta = jnp.sum(head_columns(drift, h, size), axis=1, keepdims=True)
        prob_h = prob[h]
        d_score = prob_h * (product_right(d_mix_h, value_h) - delta)
        d_score_ref[h] = d_score
        d_score_b = d_score.astype(bf16)
        d_queries.append(product(d_score_b, key_h))
        d_keys.append(product_left(d_score_b, query_h))
        d_values.append(product_left(prob_h.astype(bf16), d_mix_h))
    d_query = jnp.concatenate(d_queries, axis=1).astype(bf16)
    d_key = jnp.concatenate(d_keys, axis=1).astype(bf16)
    d_value = jnp.concatenate(d_values, axis=1).astype(bf16)
    d_qkv_ref[...] = jnp.concatenate([d_query, d_key, d_value], axis=1)
    part_ref[...] = (
        product_right(d_query, wq[...])
        + product_right(d_key, wk[...])
        + product_right(d_value, wv[...])
    )
    split_halves(part_ref, send_ref, keep_ref, place[0])


def shift_left_by_row(values):
    rows, columns = values.shape
    row_id = lax.broadcasted_iota(jnp.int32, values.shape, 0)
    step = 1
    while step < rows:
        rolled = pltpu.roll(values, columns - step, 1)
        values = jnp.where(row_id & step != 0, rolled, values)
        step *= 2
    return values


def self_grads(
    place, normed, grad_b, mix, d_qkv, d_score, back_buckets,
    send_ref, keep_ref, d_bias_ref, grad_ref, *, heads,
):
    grad_ref[...] = jnp.concatenate(
        [product_left(normed[...], d_qkv[...]), product_left(grad_b[...], mix[...])], axis=1
    )
    split_blocks(grad_ref, send_ref, keep_ref, place[1])
    bucket_id = lax.broadcasted_iota(
        jnp.int32, (d_bias_ref.shape[0], back_buckets.shape[1]), 0
    )
    hit = bucket_id == back_buckets[...]
    for h in range(heads):
        by_offset = jnp.sum(shift_left_by_row(d_score[h]), axis=0, keepdims=True)
        d_bias_ref[:, h : h + 1] = jnp.sum(
            jnp.where(hit, by_offset, 0.0), axis=1, keepdims=True
        )


def input_grad(place, own, other, x_ref, gain, grad_one, d_input_ref, d_gain_ref, part_ref):
    join_halves(part_ref, own, other, place[0])
    d_resid, d_gain = norm_pull(x_ref[...].astype(f32), gain[...], part_ref[...])
    d_gain_ref[...] = d_gain
    d_input_ref[...] = grad_one[...] + d_resid


def kernel_call(body, outs, scratch, *operands, **static):
    if static:
        body = functools.partial(body, **static)
    specs = [
        pl.BlockSpec(memory_space=pltpu.SMEM if operand.ndim == 1 else pltpu.VMEM)
        for operand in operands
    ]
    return pl.pallas_call(
        body,
        out_shape=[jax.ShapeDtypeStruct(shape, dtype) for shape, dtype in outs],
        in_specs=specs,
        out_specs=[pl.BlockSpec(memory_space=pltpu.VMEM) for unused in outs],
        scratch_shapes=[pltpu.VMEM(shape, f32) for shape in scratch],
    )(*operands)


def swap_pairs(count, stride):
    return [(i, i ^ stride) for i in range(count)]


def swap_halves(send, keep):
    count = lax.axis_size("tensor")
    total = keep + lax.ppermute(send, "tensor", swap_pairs(count, 1))
    stride = 2
    while stride < count:
        total = total + lax.ppermute(total, "tensor", swap_pairs(count, stride))
        stride *= 2
    return total, lax.ppermute(total, "tensor", swap_pairs(count, 1))


def halve_blocks(blocks, axis_name, bits, remaining):
    count = lax.axis_size(axis_name)
    index = lax.axis_index(axis_name)
    remaining = list(remaining)
    shape = blocks.shape[1:]
    for bit in bits:
        low = 2 ** remaining.index(bit)
        high = 2 ** (len(remaining) - 1 - remaining.index(bit))
        mine = (index >> bit) & 1
        view = blocks.reshape((high, 2, low) + shape)
        keep = lax.dynamic_index_in_dim(view, mine, 1, keepdims=False)
        send = lax.dynamic_index_in_dim(view, 1 - mine, 1, keepdims=False)
        received = lax.ppermute(send, axis_name, swap_pairs(count, 2**bit))
        blocks = (keep + received).reshape((high * low,) + shape)
        remaining.remove(bit)
    return blocks[0]


def bit_list(axis_name):
    return list(range(lax.axis_size(axis_name).bit_length() - 1))


def finish_blocks(send, keep, axis_name):
    bits = bit_list(axis_name)
    count = lax.axis_size(axis_name)
    blocks = keep + lax.ppermute(send, axis_name, swap_pairs(count, 1))
    return halve_blocks(blocks, axis_name, bits[1:], bits[1:])


def on_device(
    layer_input,
    encoder_states,
    output_grad,
    segments,
    buckets,
    bias_table,
    gain_self,
    self_query,
    self_key,
    self_value,
    self_out,
    gain_cross,
    cross_query,
    cross_key,
    cross_value,
    cross_out,
    gain_ff,
    ff_gate,
    ff_up,
    ff_down,
):
    rows, model = layer_input.shape
    heads = bias_table.shape[1]
    width = self_query.shape[1]
    hidden_width = ff_gate.shape[1]
    dp_count = lax.axis_size("dp")
    share = model // dp_count
    tensor_count = lax.axis_size("tensor")
    place = jnp.stack([lax.axis_index("tensor") & 1, lax.axis_index("dp") & 1]).astype(jnp.int32)
    back_buckets = jnp.roll(jnp.flip(buckets), 1).reshape(1, rows)
    gain_a = gain_self.reshape(1, model)
    gain_b = gain_cross.reshape(1, model)
    gain_c = gain_ff.reshape(1, model)
    full = (rows, model)
    half = ((rows // 2, model), f32)
    probs = (heads, rows, rows)
    pieces = ((tensor_count // 2, rows, model // tensor_count), f32)

    normed_self, qkv, prob_self, mix_self, send, keep = kernel_call(
        self_forward,
        [(full, bf16), ((rows, 3 * width), bf16), (probs, f32), ((rows, width), bf16), half, half],
        [full],
        place, layer_input, gain_a, self_query, self_key, self_value, self_out,
        segments, back_buckets, bias_table,
    )
    own, other = swap_halves(send, keep)
    (kv,) = kernel_call(
        cross_key_value,
        [((rows, 2 * width), bf16)],
        [],
        encoder_states, cross_key, cross_value,
    )
    resid_one, normed_cross, query, prob_cross, mix_cross, send, keep = kernel_call(
        cross_forward,
        [(full, f32), (full, bf16), ((rows, width), bf16), (probs, f32), ((rows, width), bf16),
         half, half],
        [full],
        place, own, other, layer_input, gain_b, cross_query, cross_out, kv,
        heads=heads,
    )
    own, other = swap_halves(send, keep)
    resid_two, normed_ff, hidden, d_pre, send, keep = kernel_call(
        ff_both,
        [(full, f32), (full, bf16), ((rows, hidden_width), bf16), ((rows, 2 * hidden_width), bf16),
         half, half],
        [full],
        place, own, other, resid_one, gain_c, ff_gate, ff_up, ff_down, output_grad,
    )
    own, other = swap_halves(send, keep)
    split = (dp_count // 2, share)
    pre_send, pre_keep, down_blocks, out_send, out_keep = kernel_call(
        ff_grads,
        [(split + (2 * hidden_width,), f32), (split + (2 * hidden_width,), f32),
         ((dp_count, share, hidden_width), f32), pieces, pieces],
        [(model, 2 * hidden_width)],
        place, normed_ff, d_pre, hidden, output_grad, ff_down,
    )
    (grad_two, grad_two_b, d_gain_ff, d_mix, d_score, d_query, send, keep) = kernel_call(
        cross_backward,
        [(full, f32), (full, bf16), ((1, model), f32), ((rows, width), bf16), (probs, bf16),
         ((rows, width), bf16), half, half],
        [full],
        place, own, other, resid_two, gain_c, output_grad, cross_out, cross_query,
        prob_cross, query, kv, mix_cross,
        heads=heads,
    )
    own, other = swap_halves(send, keep)
    cross_send, cross_keep, enc_send, enc_keep = kernel_call(
        cross_grads,
        [(split + (4 * width,), f32), (split + (4 * width,), f32), pieces, pieces],
        [(model, 4 * width)],
        place, normed_cross, encoder_states, grad_two_b, mix_cross, prob_cross, query, d_mix,
        d_score, d_query, cross_key, cross_value,
        heads=heads,
    )
    grad_one, grad_one_b, d_gain_cross, d_score_self, d_qkv, send, keep = kernel_call(
        self_backward,
        [(full, f32), (full, bf16), ((1, model), f32), (probs, f32), ((rows, 3 * width), bf16),
         half, half],
        [full],
        place, own, other, resid_one, gain_b, grad_two, self_out, self_query, self_key,
        self_value, prob_self, qkv, mix_self,
        heads=heads,
    )
    own, other = swap_halves(send, keep)
    self_send, self_keep, d_bias = kernel_call(
        self_grads,
        [(split + (4 * width,), f32), (split + (4 * width,), f32), (bias_table.shape, f32)],
        [(model, 4 * width)],
        place, normed_self, grad_one_b, mix_self, d_qkv, d_score_self, back_buckets,
        heads=heads,
    )
    d_layer_input, d_gain_self = kernel_call(
        input_grad,
        [(full, f32), ((1, model), f32)],
        [full],
        place, own, other, layer_input, gain_a, grad_one,
    )

    out_share = finish_blocks(out_send, out_keep, "tensor")
    col_width = out_share.shape[1]
    resid_cols = lax.dynamic_slice_in_dim(
        resid_two, lax.axis_index("tensor") * col_width, col_width, 1
    )
    layer_output = (resid_cols + out_share).astype(bf16)
    d_encoder_states = finish_blocks(enc_send, enc_keep, "tensor")
    dp_bits = bit_list("dp")
    down_rows = halve_blocks(down_blocks, "dp", dp_bits[1:] + dp_bits[:1], dp_bits)
    pre_rows = finish_blocks(pre_send, pre_keep, "dp")
    cross_rows = finish_blocks(cross_send, cross_keep, "dp")
    self_rows = finish_blocks(self_send, self_keep, "dp")
    small = jnp.concatenate(
        [g.reshape(dp_count, share) for g in (d_gain_self, d_gain_cross, d_gain_ff)]
        + [jnp.broadcast_to(d_bias.reshape(1, d_bias.size), (dp_count, d_bias.size))],
        axis=1,
    )
    small = halve_blocks(small, "dp", dp_bits, dp_bits)
    return (
        layer_output,
        d_layer_input,
        d_encoder_states,
        small[3 * share :].reshape(d_bias.shape),
        small[:share],
        self_rows[:, :width],
        self_rows[:, width : 2 * width],
        self_rows[:, 2 * width : 3 * width],
        jnp.transpose(self_rows[:, 3 * width :]),
        small[share : 2 * share],
        cross_rows[:, 2 * width : 3 * width],
        cross_rows[:, :width],
        cross_rows[:, width : 2 * width],
        jnp.transpose(cross_rows[:, 3 * width :]),
        small[2 * share : 3 * share],
        pre_rows[:, :hidden_width],
        pre_rows[:, hidden_width:],
        jnp.transpose(down_rows),
    )


def solution(mesh):
    in_specs = (
        P("dp", None),
        P("dp", None),
        P("dp", None),
        P("dp", None),
        P(),
        P(None, "tensor"),
        P(),
        P(None, "tensor"),
        P(None, "tensor"),
        P(None, "tensor"),
        P("tensor", None),
        P(),
        P(None, "tensor"),
        P(None, "tensor"),
        P(None, "tensor"),
        P("tensor", None),
        P(),
        P(None, "tensor"),
        P(None, "tensor"),
        P("tensor", None),
    )
    out_specs = (
        P("dp", "tensor"),
        P("dp", None),
        P("dp", "tensor"),
        P(None, "tensor"),
        P("dp"),
        P("dp", "tensor"),
        P("dp", "tensor"),
        P("dp", "tensor"),
        P("tensor", "dp"),
        P("dp"),
        P("dp", "tensor"),
        P("dp", "tensor"),
        P("dp", "tensor"),
        P("tensor", "dp"),
        P("dp"),
        P("dp", "tensor"),
        P("dp", "tensor"),
        P("tensor", "dp"),
    )
    return jax.shard_map(
        on_device, mesh=mesh, in_specs=in_specs, out_specs=out_specs, check_vma=False
    )
```

```python
import functools
import math

import jax
import jax.numpy as jnp
from jax import lax
from jax.experimental import pallas as pl
from jax.experimental.pallas import tpu as pltpu
from jax.sharding import PartitionSpec as P


epsilon = 1e-06
masked_value = -1000000000.0
gelu_rate = 0.7978845608028654
gelu_cube = 0.044715
f32 = jnp.float32
bf16 = jnp.bfloat16
spare_bytes = 12 * 2**20


def product(left, right):
    return jnp.dot(left, right, preferred_element_type=f32)


def product_left(left, right):
    return lax.dot_general(left, right, (((0,), (0,)), ((), ())), preferred_element_type=f32)


def product_right(left, right):
    return lax.dot_general(left, right, (((1,), (1,)), ((), ())), preferred_element_type=f32)


def inverse_rms(values):
    return lax.rsqrt(jnp.mean(values * values, axis=-1, keepdims=True) + epsilon)


def norm_pull(values, gain_row, cotangent):
    scale = inverse_rms(values)
    weighted = cotangent * gain_row
    mean_part = jnp.mean(weighted * values, axis=-1, keepdims=True)
    d_values = scale * weighted - values * (scale * scale * scale * mean_part)
    d_gain = jnp.sum(cotangent * values * scale, axis=0, keepdims=True)
    return d_values, d_gain


def core_bit():
    return lax.axis_index("tensor") & 1


def pair_bit():
    return lax.axis_index("dp") & 1


def as_row(ref):
    return ref[...].reshape(1, ref.shape[0])


def head_columns(values, head, width):
    return values[:, head * width : (head + 1) * width]


def split_halves(part_ref, send_ref, keep_ref, bit):
    half = keep_ref.shape[0]
    send_ref[...] = part_ref[pl.ds((1 - bit) * half, half), :]
    keep_ref[...] = part_ref[pl.ds(bit * half, half), :]


def join_halves(full_ref, own_ref, other_ref, bit):
    half = own_ref.shape[0]
    full_ref[pl.ds(bit * half, half), :] = own_ref[...]
    full_ref[pl.ds((1 - bit) * half, half), :] = other_ref[...]


def split_blocks(grad_ref, send_ref, keep_ref, bit):
    pairs, rows, _ = keep_ref.shape
    for pair in range(pairs):
        if rows % 8 == 0:
            start = 2 * pair * rows
            send_ref[pair] = grad_ref[pl.ds(pl.multiple_of(start + (1 - bit) * rows, 8), rows), :]
            keep_ref[pair] = grad_ref[pl.ds(pl.multiple_of(start + bit * rows, 8), rows), :]
        else:
            first = grad_ref[2 * pair * rows : (2 * pair + 1) * rows, :]
            second = grad_ref[(2 * pair + 1) * rows : (2 * pair + 2) * rows, :]
            send_ref[pair] = jnp.where(bit == 0, second, first)
            keep_ref[pair] = jnp.where(bit == 0, first, second)


def bucket_hits(buckets, count):
    size = buckets.shape[0]
    row = jnp.broadcast_to(as_row(buckets), (8, size)).astype(f32).astype(bf16)
    source = lax.broadcasted_iota(jnp.int32, (size, size), 0)
    target = lax.broadcasted_iota(jnp.int32, (size, size), 1)
    mirror = (source + target == size) | (source + target == 0)
    turned = product(row, mirror.astype(f32).astype(bf16))[:1]
    bucket_id = lax.broadcasted_iota(jnp.int32, (count, size), 0).astype(f32)
    return (bucket_id == turned).astype(f32)


def softmax_rows(scores):
    exp_scores = jnp.exp(scores - jnp.max(scores, axis=-1, keepdims=True))
    return exp_scores / jnp.sum(exp_scores, axis=-1, keepdims=True)


def self_forward(
    x_ref, gain, wq, wk, wv, wo, seg, buckets, table,
    normed_ref, qkv_ref, prob_ref, mix_ref, send_ref, keep_ref, part_ref,
):
    heads = table.shape[0]
    width = wq.shape[0]
    size = width // heads
    rows = x_ref.shape[0]
    x = x_ref[...].astype(f32)
    normed = (x * inverse_rms(x) * as_row(gain)).astype(bf16)
    normed_ref[...] = normed
    query = product_right(normed, wq[...]).astype(bf16)
    key_rows = product_right(normed, wk[...]).astype(bf16)
    values = product_right(normed, wv[...]).astype(bf16)
    qkv_ref[...] = jnp.concatenate([query, key_rows, values], axis=1)
    row_id = lax.broadcasted_iota(jnp.int32, (rows, rows), 0)
    col_id = lax.broadcasted_iota(jnp.int32, (rows, rows), 1)
    seg_row = seg[...]
    seg_col = jnp.sum(jnp.where(row_id == col_id, seg_row, 0), axis=1, keepdims=True)
    allowed = (row_id >= col_id) & (seg_col == seg_row)
    hit = bucket_hits(buckets, table.shape[1])
    table_f = table[...].astype(f32)
    by_offset = jnp.dot(table_f, hit, precision=lax.Precision.HIGHEST)
    mixes = []
    for h in range(heads):
        pattern = by_offset[h : h + 1]
        bias = pltpu.roll(
            jnp.broadcast_to(pattern, (rows, rows)), 0, 1, stride=1, stride_axis=0
        )
        scores = product_right(head_columns(query, h, size), head_columns(key_rows, h, size))
        prob = softmax_rows(jnp.where(allowed, scores + bias, masked_value))
        prob_ref[h] = prob
        mixes.append(product(prob.astype(bf16), head_columns(values, h, size)))
    mix = jnp.concatenate(mixes, axis=1).astype(bf16)
    mix_ref[...] = mix
    part_ref[...] = product(mix, wo[...])
    split_halves(part_ref, send_ref, keep_ref, core_bit())


def cross_forward(
    own, other, x_ref, gain, wq, wo, kv,
    resid_ref, normed_ref, query_ref, prob_ref, mix_ref, send_ref, keep_ref, part_ref, *, heads,
):
    width = wq.shape[0]
    size = width // heads
    join_halves(part_ref, own, other, core_bit())
    resid = x_ref[...].astype(f32) + part_ref[...]
    resid_ref[...] = resid
    normed = (resid * inverse_rms(resid) * as_row(gain)).astype(bf16)
    normed_ref[...] = normed
    query = product_right(normed, wq[...]).astype(bf16)
    query_ref[...] = query
    mixes = []
    for h in range(heads):
        key_h = kv[:, h * size : (h + 1) * size]
        value_h = kv[:, width + h * size : width + (h + 1) * size]
        prob = softmax_rows(product_right(head_columns(query, h, size), key_h))
        prob_ref[h] = prob
        mixes.append(product(prob.astype(bf16), value_h))
    mix = jnp.concatenate(mixes, axis=1).astype(bf16)
    mix_ref[...] = mix
    part_ref[...] = product(mix, wo[...])
    split_halves(part_ref, send_ref, keep_ref, core_bit())


def cross_key_value(enc, wk, wv, kv_ref):
    rows = enc[...]
    kv_ref[...] = jnp.concatenate(
        [product_right(rows, wk[...]).astype(bf16), product_right(rows, wv[...]).astype(bf16)],
        axis=1,
    )


def ff_both(
    own, other, resid_one, gain, wg, wu, wd, out_grad,
    resid_ref, normed_ref, hidden_ref, d_pre_ref, send_ref, keep_ref, part_ref,
):
    join_halves(part_ref, own, other, core_bit())
    resid = resid_one[...] + part_ref[...]
    resid_ref[...] = resid
    normed = (resid * inverse_rms(resid) * as_row(gain)).astype(bf16)
    normed_ref[...] = normed
    gate = product(normed, wg[...])
    up = product(normed, wu[...])
    d_hidden = product_right(out_grad[...], wd[...])
    square = gate * gate
    bend = jnp.tanh(gelu_rate * (gate + gelu_cube * (square * gate)))
    activ = 0.5 * gate * (1.0 + bend)
    slope = 0.5 * (1.0 + bend) + 0.5 * gate * (1.0 - bend * bend) * (
        gelu_rate * (1.0 + 3.0 * gelu_cube * square)
    )
    hidden_ref[...] = (activ * up).astype(bf16)
    d_gate = (d_hidden * up * slope).astype(bf16)
    d_up = (d_hidden * activ).astype(bf16)
    width = d_gate.shape[1]
    d_pre_ref[:, :width] = d_gate
    d_pre_ref[:, width:] = d_up
    part_ref[...] = product_right(d_gate, wg[...]) + product_right(d_up, wu[...])
    split_halves(part_ref, send_ref, keep_ref, core_bit())


def ff_pre_grads(
    normed, d_pre, gate_send, gate_keep, up_send, up_keep, grad_ref,
):
    width = grad_ref.shape[1]
    grad_ref[...] = product_left(normed[...], d_pre[:, :width])
    split_blocks(grad_ref, gate_send, gate_keep, pair_bit())
    grad_ref[...] = product_left(normed[...], d_pre[:, width:])
    split_blocks(grad_ref, up_send, up_keep, pair_bit())


def ff_down_grad(out_grad, hidden, down_ref):
    down = product_left(out_grad[...], hidden[...])
    blocks, rows, _ = down_ref.shape
    for block in range(blocks):
        down_ref[block] = down[block * rows : (block + 1) * rows, :]


def ff_output(hidden, wd, resid, out_send, out_keep, part_ref, resid_ref):
    part_ref[...] = lax.dot_general(
        wd[...], hidden[...], (((0,), (1,)), ((), ())), preferred_element_type=f32
    )
    split_blocks(part_ref, out_send, out_keep, core_bit())
    resid_ref[...] = jnp.transpose(resid[...])
    index = lax.axis_index("tensor")
    rows = out_keep.shape[1]
    out_keep[index >> 1] += resid_ref[pl.ds(pl.multiple_of(index * rows, 8), rows), :]


def cross_backward(
    own, other, resid_two, gain, out_grad, wo, wq, prob, query, kv, mix,
    grad_ref, grad_b_ref, d_gain_ref, d_mix_ref, d_score_ref, d_query_ref, send_ref, keep_ref,
    part_ref, *, heads,
):
    width = wq.shape[0]
    size = width // heads
    join_halves(part_ref, own, other, core_bit())
    d_resid, d_gain = norm_pull(resid_two[...], as_row(gain), part_ref[...])
    d_gain_ref[...] = d_gain
    grad = out_grad[...].astype(f32) + d_resid
    grad_ref[...] = grad
    grad_b = grad.astype(bf16)
    grad_b_ref[...] = grad_b
    d_mix = product_right(grad_b, wo[...]).astype(bf16)
    d_mix_ref[...] = d_mix
    drift = d_mix.astype(f32) * mix[...].astype(f32)
    d_queries = []
    for h in range(heads):
        key_h = kv[:, h * size : (h + 1) * size]
        value_h = kv[:, width + h * size : width + (h + 1) * size]
        delta = jnp.sum(head_columns(drift, h, size), axis=1, keepdims=True)
        d_prob = product_right(head_columns(d_mix, h, size), value_h)
        d_score = (prob[h] * (d_prob - delta)).astype(bf16)
        d_score_ref[h] = d_score
        d_queries.append(product(d_score, key_h))
    d_query = jnp.concatenate(d_queries, axis=1).astype(bf16)
    d_query_ref[...] = d_query
    part_ref[...] = product(d_query, wq[...])
    split_halves(part_ref, send_ref, keep_ref, core_bit())


def cross_grads(
    normed, enc, grad_b, mix, prob, query, d_mix, d_score, d_query, wk, wv,
    send_ref, keep_ref, enc_send, enc_keep, grad_ref, part_ref, *, heads,
):
    width = wk.shape[0]
    size = width // heads
    d_keys = []
    d_values = []
    for h in range(heads):
        d_keys.append(product_left(d_score[h], query[:, h * size : (h + 1) * size]))
        d_values.append(product_left(prob[h].astype(bf16), d_mix[:, h * size : (h + 1) * size]))
    d_key = jnp.concatenate(d_keys, axis=1).astype(bf16)
    d_value = jnp.concatenate(d_values, axis=1).astype(bf16)
    part_ref[...] = lax.dot_general(
        wk[...], d_key, (((0,), (1,)), ((), ())), preferred_element_type=f32
    ) + lax.dot_general(wv[...], d_value, (((0,), (1,)), ((), ())), preferred_element_type=f32)
    split_blocks(part_ref, enc_send, enc_keep, core_bit())
    grad_ref[:, : 2 * width] = product_left(enc[...], jnp.concatenate([d_key, d_value], axis=1))
    grad_ref[:, 2 * width :] = jnp.concatenate(
        [product_left(normed[...], d_query[...]), product_left(grad_b[...], mix[...])], axis=1
    )
    split_blocks(grad_ref, send_ref, keep_ref, pair_bit())


def self_backward(
    own, other, resid_one, gain, grad_two, wo, wq, wk, wv, prob, qkv, mix,
    grad_ref, grad_b_ref, d_gain_ref, d_score_ref, d_qkv_ref, send_ref, keep_ref,
    part_ref, *, heads,
):
    width = wq.shape[0]
    size = width // heads
    join_halves(part_ref, own, other, core_bit())
    d_resid, d_gain = norm_pull(resid_one[...], as_row(gain), part_ref[...])
    d_gain_ref[...] = d_gain
    grad = grad_two[...] + d_resid
    grad_ref[...] = grad
    grad_b = grad.astype(bf16)
    grad_b_ref[...] = grad_b
    d_mix = product_right(grad_b, wo[...]).astype(bf16)
    drift = d_mix.astype(f32) * mix[...].astype(f32)
    d_queries = []
    d_keys = []
    d_values = []
    for h in range(heads):
        query_h = qkv[:, h * size : (h + 1) * size]
        key_h = qkv[:, width + h * size : width + (h + 1) * size]
        value_h = qkv[:, 2 * width + h * size : 2 * width + (h + 1) * size]
        d_mix_h = head_columns(d_mix, h, size)
        delta = jnp.sum(head_columns(drift, h, size), axis=1, keepdims=True)
        prob_h = prob[h]
        d_score = prob_h * (product_right(d_mix_h, value_h) - delta)
        d_score_ref[h] = d_score
        d_score_b = d_score.astype(bf16)
        d_queries.append(product(d_score_b, key_h))
        d_keys.append(product_left(d_score_b, query_h))
        d_values.append(product_left(prob_h.astype(bf16), d_mix_h))
    d_query = jnp.concatenate(d_queries, axis=1).astype(bf16)
    d_key = jnp.concatenate(d_keys, axis=1).astype(bf16)
    d_value = jnp.concatenate(d_values, axis=1).astype(bf16)
    d_qkv_ref[...] = jnp.concatenate([d_query, d_key, d_value], axis=1)
    part_ref[...] = (
        product(d_query, wq[...]) + product(d_key, wk[...]) + product(d_value, wv[...])
    )
    split_halves(part_ref, send_ref, keep_ref, core_bit())


def shift_left_by_row(values):
    rows, columns = values.shape
    row_id = lax.broadcasted_iota(jnp.int32, values.shape, 0)
    step = 1
    while step < rows:
        rolled = pltpu.roll(values, columns - step, 1)
        values = jnp.where(row_id & step != 0, rolled, values)
        step *= 2
    return values


def self_grads(
    normed, grad_b, mix, d_qkv, d_score, buckets,
    send_ref, keep_ref, rest_ref, d_bias_ref, grad_ref, *, heads,
):
    width = mix.shape[1]
    grad_ref[...] = product_left(normed[...], d_qkv[:, : 2 * width])
    split_blocks(grad_ref, send_ref, keep_ref, pair_bit())
    rest = jnp.concatenate(
        [
            product_left(normed[...], d_qkv[:, 2 * width :]),
            product_left(grad_b[...], mix[...]),
        ],
        axis=1,
    )
    blocks, rows, _ = rest_ref.shape
    for block in range(blocks):
        rest_ref[block] = rest[block * rows : (block + 1) * rows, :]
    hit = bucket_hits(buckets, d_bias_ref.shape[1])
    by_offset = jnp.concatenate(
        [
            jnp.sum(shift_left_by_row(d_score[h]), axis=0, keepdims=True)
            for h in range(heads)
        ],
        axis=0,
    )
    d_bias_ref[...] = lax.dot_general(
        by_offset, hit, (((1,), (1,)), ((), ())), precision=lax.Precision.HIGHEST
    )


def input_grad(
    own, other, x_ref, gain, grad_one, d_gain_cross, d_gain_ff, d_bias,
    d_input_ref, small_ref, part_ref,
):
    join_halves(part_ref, own, other, core_bit())
    d_resid, d_gain = norm_pull(x_ref[...].astype(f32), as_row(gain), part_ref[...])
    d_input_ref[...] = grad_one[...] + d_resid
    blocks = small_ref.shape[0]
    share = d_gain.shape[1] // blocks
    for place, row in enumerate((d_gain, d_gain_cross[...], d_gain_ff[...])):
        for block in range(blocks):
            small_ref[block : block + 1, place * share : (place + 1) * share] = row[
                :, block * share : (block + 1) * share
            ]
    heads, count = d_bias.shape
    for h in range(heads):
        small_ref[:, 3 * share + h * count : 3 * share + (h + 1) * count] = jnp.broadcast_to(
            d_bias[h : h + 1, :], (blocks, count)
        )


def split_columns(keep, received, *out_refs):
    total = keep[...] + received[...]
    start = 0
    for out_ref in out_refs:
        out_ref[...] = total[:, start : start + out_ref.shape[1]]
        start += out_ref.shape[1]


def kernel_call(body, outs, scratch, *operands, **static):
    if static:
        body = functools.partial(body, **static)

    def size_of(shape, dtype):
        lanes = -(-shape[-1] // 128) * 128
        return math.prod(shape[:-1]) * lanes * jnp.dtype(dtype).itemsize

    used = sum(size_of(shape, dtype) for shape, dtype in outs)
    used += sum(size_of(operand.shape, operand.dtype) for operand in operands)
    used += sum(size_of(shape, f32) for shape in scratch)
    vmem = pl.BlockSpec(memory_space=pltpu.VMEM)
    return pl.pallas_call(
        body,
        out_shape=[jax.ShapeDtypeStruct(shape, dtype) for shape, dtype in outs],
        in_specs=[vmem for unused in operands],
        out_specs=[vmem for unused in outs],
        scratch_shapes=[pltpu.VMEM(shape, f32) for shape in scratch],
        compiler_params=pltpu.CompilerParams(vmem_limit_bytes=used + spare_bytes),
    )(*operands)


def after(value, *anchors):
    return lax.optimization_barrier((value,) + anchors)[0]


def swap(value, axis_name, stride):
    count = lax.axis_size(axis_name)
    return lax.ppermute(value, axis_name, [(i, i ^ stride) for i in range(count)])


def swap_halves(send, keep, filler=None, before=()):
    count = lax.axis_size("tensor")
    received = swap(send, "tensor", 1)
    if before:
        received = after(received, *before)
    total = keep + received
    extra = None
    stride = 2
    while stride < count:
        received = swap(total, "tensor", stride)
        if filler is not None:
            extra, anchors = filler(total)
            received = after(received, *anchors)
            filler = None
        total = total + received
        stride *= 2
    return total, swap(total, "tensor", 1), extra


class BlockSum:
    def __init__(self, axis_name, bits, blocks=None, send=None, keep=None):
        self.axis_name = axis_name
        self.bits = list(bits)
        self.left = sorted(bits)
        if blocks is not None:
            (keep,), (send,) = self.choose(blocks)
        self.launch(send, keep)

    def choose(self, *parts):
        bit = self.bits[0]
        place = self.left.index(bit)
        low = 2**place
        high = 2 ** (len(self.left) - 1 - place)
        mine = (lax.axis_index(self.axis_name) >> bit) & 1

        def pick(part, which):
            shape = part.shape[1:]
            view = part.reshape((high, 2, low) + shape)
            picked = lax.dynamic_index_in_dim(view, which, 1, keepdims=False)
            return picked.reshape((high * low,) + shape)

        return [pick(part, mine) for part in parts], [pick(part, 1 - mine) for part in parts]

    def launch(self, send, keep):
        self.keep = keep
        self.received = swap(send, self.axis_name, 2 ** self.bits[0])
        self.left.remove(self.bits.pop(0))

    def advance(self, *anchors):
        received = after(self.received, *anchors) if anchors else self.received
        kept, sent = self.choose(self.keep, received)
        self.launch(sent[0] + sent[1], kept[0] + kept[1])
        return self.keep

    def finish(self, *anchors):
        while self.bits:
            self.advance(*anchors)
            anchors = ()
        received = after(self.received, *anchors) if anchors else self.received
        return self.keep[0], received[0]


def bit_list(axis_name):
    return list(range(lax.axis_size(axis_name).bit_length() - 1))


def on_device(
    layer_input,
    encoder_states,
    output_grad,
    segments,
    buckets,
    bias_table,
    gain_self,
    self_query,
    self_key,
    self_value,
    self_out,
    gain_cross,
    cross_query,
    cross_key,
    cross_value,
    cross_out,
    gain_ff,
    ff_gate,
    ff_up,
    ff_down,
):
    rows, model = layer_input.shape
    heads = bias_table.shape[1]
    width = self_query.shape[1]
    hidden_width = ff_gate.shape[1]
    dp_count = lax.axis_size("dp")
    tensor_count = lax.axis_size("tensor")
    share = model // dp_count
    dp_bits = bit_list("dp")
    tensor_bits = bit_list("tensor")
    high_first = dp_bits[1:] + dp_bits[:1]
    table_rows = bias_table.T
    query_rows, key_rows, value_rows = self_query.T, self_key.T, self_value.T
    cross_query_rows, cross_key_rows, cross_value_rows = cross_query.T, cross_key.T, cross_value.T
    full = (rows, model)
    half = ((rows // 2, model), f32)
    probs = (heads, rows, rows)
    pieces = ((tensor_count // 2, model // tensor_count, rows), f32)
    split = (dp_count // 2, share)

    normed_self, qkv, prob_self, mix_self, send, keep = kernel_call(
        self_forward,
        [(full, bf16), ((rows, 3 * width), bf16), (probs, f32), ((rows, width), bf16), half, half],
        [full],
        layer_input, gain_self, query_rows, key_rows, value_rows, self_out,
        segments, buckets, table_rows,
    )

    def fill_self(anchor):
        (kv,) = kernel_call(
            cross_key_value,
            [((rows, 2 * width), bf16)],
            [],
            after(encoder_states, anchor), cross_key_rows, cross_value_rows,
        )
        return kv, (kv,)

    own, other, kv = swap_halves(send, keep, fill_self)
    resid_one, normed_cross, query, prob_cross, mix_cross, send, keep = kernel_call(
        cross_forward,
        [(full, f32), (full, bf16), ((rows, width), bf16), (probs, f32), ((rows, width), bf16),
         half, half],
        [full],
        own, other, layer_input, gain_cross, cross_query_rows, cross_out, kv,
        heads=heads,
    )
    own, other, _ = swap_halves(send, keep)
    resid_two, normed_ff, hidden, d_pre, send, keep = kernel_call(
        ff_both,
        [(full, f32), (full, bf16), ((rows, hidden_width), bf16), ((rows, 2 * hidden_width), bf16),
         half, half],
        [full],
        own, other, resid_one, gain_ff, ff_gate, ff_up, ff_down, output_grad,
    )
    piece = (split + (hidden_width,), f32)
    gate_send, gate_keep, up_send, up_keep = kernel_call(
        ff_pre_grads,
        [piece, piece, piece, piece],
        [(model, hidden_width)],
        normed_ff, d_pre,
    )
    gate_sum = BlockSum("dp", dp_bits, send=gate_send, keep=gate_keep)
    up_sum = BlockSum("dp", dp_bits, send=up_send, keep=up_keep)

    def fill_ff(anchor):
        (down_blocks,) = kernel_call(
            ff_down_grad,
            [((dp_count, share, hidden_width), f32)],
            [],
            after(output_grad, anchor), hidden,
        )
        down_sum = BlockSum("dp", high_first, blocks=down_blocks)
        out_send, out_keep = kernel_call(
            ff_output,
            [pieces, pieces],
            [(model, rows), (model, rows)],
            after(hidden, down_blocks), ff_down, resid_two,
        )
        out_sum = BlockSum("tensor", tensor_bits, send=out_send, keep=out_keep)
        return (down_sum, out_sum), (down_sum.keep, out_keep)

    own, other, (down_sum, out_sum) = swap_halves(send, keep, fill_ff, (gate_send,))
    grad_two, grad_two_b, d_gain_ff, d_mix, d_score, d_query, send, keep = kernel_call(
        cross_backward,
        [(full, f32), (full, bf16), ((1, model), f32), ((rows, width), bf16), (probs, bf16),
         ((rows, width), bf16), half, half],
        [full],
        own, other, resid_two, gain_ff, output_grad, cross_out, cross_query_rows,
        prob_cross, query, kv, mix_cross,
        heads=heads,
    )
    out_sum.advance(grad_two)

    def fill_cross(anchor):
        moved = [down_sum.advance(anchor), gate_sum.advance(anchor)]
        cross_send, cross_keep, enc_send, enc_keep = kernel_call(
            cross_grads,
            [(split + (4 * width,), f32), (split + (4 * width,), f32), pieces, pieces],
            [(model, 4 * width), (model, rows)],
            normed_cross, encoder_states, grad_two_b, mix_cross, prob_cross, query, d_mix,
            after(d_score, *moved), d_query, cross_key_rows, cross_value_rows,
            heads=heads,
        )
        cross_sum = BlockSum("dp", dp_bits, send=cross_send, keep=cross_keep)
        enc_sum = BlockSum("tensor", tensor_bits, send=enc_send, keep=enc_keep)
        return (cross_sum, enc_sum), (cross_keep,)

    own, other, (cross_sum, enc_sum) = swap_halves(send, keep, fill_cross)
    grad_one, grad_one_b, d_gain_cross, d_score_self, d_qkv, send, keep = kernel_call(
        self_backward,
        [(full, f32), (full, bf16), ((1, model), f32), (probs, f32), ((rows, 3 * width), bf16),
         half, half],
        [full],
        own, other, resid_one, gain_cross, grad_two, self_out, query_rows, key_rows,
        value_rows, prob_self, qkv, mix_self,
        heads=heads,
    )
    enc_sum.advance(grad_one)

    def fill_input(anchor):
        moved = [chain.advance(anchor) for chain in (down_sum, gate_sum, up_sum)]
        self_send, self_keep, rest_blocks, d_bias = kernel_call(
            self_grads,
            [(split + (2 * width,), f32), (split + (2 * width,), f32),
             ((dp_count, share, 2 * width), f32), (table_rows.shape, f32)],
            [(model, 2 * width)],
            after(normed_self, *moved), grad_one_b, mix_self, d_qkv, d_score_self, buckets,
            heads=heads,
        )
        self_sum = BlockSum("dp", dp_bits, send=self_send, keep=self_keep)
        rest_sum = BlockSum("dp", high_first, blocks=rest_blocks)
        return (self_sum, rest_sum, d_bias), (self_keep, rest_sum.keep)

    own, other, (self_sum, rest_sum, d_bias) = swap_halves(send, keep, fill_input)
    d_layer_input, small = kernel_call(
        input_grad,
        [(full, f32), ((dp_count, 3 * share + d_bias.size), f32)],
        [full],
        own, other, layer_input, gain_self, grad_one, d_gain_cross, d_gain_ff, d_bias,
    )
    small_sum = BlockSum("dp", dp_bits, blocks=small)

    def columns(chain, pieces, *anchors):
        kept, received = chain.finish(*anchors)
        return kernel_call(
            split_columns, [((share, width), f32) for _ in range(pieces)], [], kept, received
        )

    kept, received = out_sum.finish(d_layer_input)
    layer_output = (kept + received).astype(bf16).T
    kept, received = enc_sum.finish(d_layer_input)
    d_encoder_states = (kept + received).T
    kept, received = gate_sum.finish(d_layer_input)
    gate_rows = kept + received
    up_sum.advance(gate_rows)
    kept, received = down_sum.finish(gate_rows)
    down_rows = kept + received
    small_sum.advance(down_rows)
    cross_sum.advance(down_rows)
    kept, received = up_sum.finish(cross_sum.keep)
    up_rows = kept + received
    rest_sum.advance(up_rows)
    small_sum.advance(rest_sum.keep)
    self_sum.advance(rest_sum.keep)
    d_cross_key, d_cross_value, d_cross_query, d_cross_out = columns(cross_sum, 4, self_sum.keep)
    d_self_value, d_self_out = columns(rest_sum, 2, d_cross_out)
    kept, received = small_sum.finish(d_cross_out)
    small = kept + received
    d_self_query, d_self_key = columns(self_sum, 2, d_self_out)
    return (
        layer_output,
        d_layer_input,
        d_encoder_states,
        small[3 * share :].reshape(table_rows.shape).T,
        small[:share],
        d_self_query,
        d_self_key,
        d_self_value,
        d_self_out.T,
        small[share : 2 * share],
        d_cross_query,
        d_cross_key,
        d_cross_value,
        d_cross_out.T,
        small[2 * share : 3 * share],
        gate_rows,
        up_rows,
        down_rows.T,
    )


def solution(mesh):
    in_specs = (
        P("dp", None),
        P("dp", None),
        P("dp", None),
        P("dp", None),
        P(),
        P(None, "tensor"),
        P(),
        P(None, "tensor"),
        P(None, "tensor"),
        P(None, "tensor"),
        P("tensor", None),
        P(),
        P(None, "tensor"),
        P(None, "tensor"),
        P(None, "tensor"),
        P("tensor", None),
        P(),
        P(None, "tensor"),
        P(None, "tensor"),
        P("tensor", None),
    )
    out_specs = (
        P("dp", "tensor"),
        P("dp", None),
        P("dp", "tensor"),
        P(None, "tensor"),
        P("dp"),
        P("dp", "tensor"),
        P("dp", "tensor"),
        P("dp", "tensor"),
        P("tensor", "dp"),
        P("dp"),
        P("dp", "tensor"),
        P("dp", "tensor"),
        P("dp", "tensor"),
        P("tensor", "dp"),
        P("dp"),
        P("dp", "tensor"),
        P("dp", "tensor"),
        P("tensor", "dp"),
    )
    return jax.shard_map(
        on_device, mesh=mesh, in_specs=in_specs, out_specs=out_specs, check_vma=False
    )
```
